32 devices in a mesh: dp: 8 (over y, x, core), tensor: 4 (over z).
Axes of the slice: x: 2, y: 2, z: 4, core: 2. Of those that a mesh axis runs over, the one named last changes fastest.
Arguments:
- tokens: bfloat16 [8, 1024, 768], P('dp', 'tensor'), may hold values from -30 to 30
- segment_ids: int32 [8, 1024], P('dp'), may hold values from 0 to 3, never falling along the last dimension, each value on 1 to 512 neighbouring positions
- qkv_weight: bfloat16 [3, 768, 768], P(None, 'dp', 'tensor'), may hold values from -1 to 1
- out_weight: bfloat16 [768, 768], P('tensor', 'dp'), may hold values from -0.875 to 0.875
- in_weight: bfloat16 [768, 3072], P('dp', 'tensor'), may hold values from -0.21875 to 0.21875
- down_weight: bfloat16 [3072, 768], P('tensor', 'dp'), may hold values from -0.109375 to 0.109375
- qv_bias: bfloat16 [2, 4, 192], P(None, 'tensor', 'dp'), may hold values from -3 to 3
- hidden_bias: bfloat16 [4, 768], P('tensor', 'dp'), may hold values from -3 to 3
- norm_vectors: float32 [6, 768], P(None, ('dp', 'tensor')), may hold values from -2 to 2
- cotangent: bfloat16 [8, 1024, 768], P('dp', 'tensor'), may hold values from -6 to 6
Outputs:
- layer_out: bfloat16 [8, 1024, 768], P('dp', 'tensor')
- tokens_grad: bfloat16 [8, 1024, 768], P('dp', 'tensor')
- qkv_grad: float32 [3, 768, 768], P(None, 'dp', 'tensor')
- out_grad: float32 [768, 768], P('tensor', 'dp')
- in_grad: float32 [768, 3072], P('dp', 'tensor')
- down_grad: float32 [3072, 768], P('tensor', 'dp')
- qv_bias_grad: float32 [2, 4, 192], P(None, 'tensor', 'dp')
- hidden_bias_grad: float32 [4, 768], P('tensor', 'dp')
- vectors_grad: float32 [6, 768], P(None, ('dp', 'tensor'))
The draws below stay inside these ranges and needn't reach their ends.
Inputs may be any that keep to these rules, and one draw needn't show every extreme that they name: `segment_ids`: segment ids never fall along a sequence; each document holds 1 to 512 tokens, one exactly 512.
All inputs are finite; a program needn't handle non-finite values.
Results may differ from the reference program's by a relative error of at most 0.028.
The reference program's roundings to bfloat16 on the way count: a program that leaves them out, or rounds other values in their place, can miss the bound.
Values may be sent and summed in bfloat16 or wider, within the bound.
A program may use at most 128 MiB of HBM per device.

```python
import math
import jax
import jax.numpy as jnp
import numpy as np
from jax import lax

D = 768
HEADS = 12
DH = 64
FF = 3072
LEN = 1024
SEQS_ALL = 8
N_TENSOR = 4


def draw_tokens(key, part):
    key_base = jax.random.fold_in(key, 0)
    drawn = jax.random.normal(key_base, (SEQS_ALL, LEN, D), jnp.float32)
    return jnp.clip(drawn, -5.0, 5.0).astype(jnp.bfloat16)


def draw_qkv_weight(key, part):
    drawn = jax.random.normal(key, (3, D, D), jnp.float32)
    return (jnp.clip(drawn, -6.0, 6.0) * D ** (-0.5)).astype(jnp.bfloat16)


def draw_norm_vectors(key, part):
    drawn = jax.random.normal(key, (6, D), jnp.float32)
    centers = jnp.array([0.0, 1.0, 0.0, 0.0, 1.0, 0.0], jnp.float32)[:, None]
    spread = jnp.array([0.5, 0.15, 0.5, 0.5, 0.15, 0.5], jnp.float32)[:, None]
    return centers + spread * jnp.clip(drawn, -3.0, 3.0)


def block_levels(stream_key, shape, pieces, smallest, high):
    loudness, own = 1.0, jax.random.fold_in(stream_key, 6)
    for axis_at, parts in pieces:
        draws = jnp.exp(jax.random.uniform(jax.random.fold_in(own, axis_at), (parts,), jnp.float32, smallest / len(pieces), high / len(pieces)))
        loudness = loudness * jnp.repeat(draws, shape[axis_at] // parts).reshape([-1 if axis == axis_at else 1 for axis in range(len(shape))])
    return loudness


def length_profile(amount, total, bound, skew):
    portions = [(1 << 20) // math.isqrt(grade ** skew) + 1 for grade in range(2, amount + 1)]
    surplus, given = total - bound - (amount - 1), [1] * (amount - 1)
    while surplus > 0:
        movable = [i for i in range(amount - 1) if given[i] < bound]
        pool, remaining = sum([portions[i] for i in movable]), surplus
        for i in movable:
            more = min(bound - given[i], max(1, remaining * portions[i] // pool), surplus)
            given[i] = given[i] + more
            surplus = surplus - more
    return np.array([bound] + given)


def ragged_sizes(key, amount, total, bound, slope):
    if amount == 2:
        one = jax.random.randint(key, (), max(1, total - bound), min(bound, total - 1) + 1)
        return jnp.stack([one, total - one])
    lengths = jnp.asarray(length_profile(amount, total, bound, slope), jnp.int32)
    twos = (amount - 1) // 2
    source_of, sink = lengths[1:1 + 2 * twos:2], lengths[2:2 + 2 * twos:2]
    margin = jnp.minimum(source_of - 1, bound - sink)
    moved = jax.random.randint(jax.random.fold_in(key, 1), (twos,), 0, 1 << 20) % (margin + 1)
    lengths = lengths.at[1:1 + 2 * twos:2].set(source_of - moved).at[2:2 + 2 * twos:2].set(sink + moved)
    return lengths[jax.random.permutation(jax.random.fold_in(key, 2), amount)]


def bell_draw(own_key, shape, deviation, bound, pieces=(), kind=jnp.bfloat16):
    result = jax.random.normal(own_key, shape, jnp.float32) * deviation
    if len(pieces) > 0:
        result = block_levels(own_key, shape, pieces, -0.22, 0.18) * result
    return jnp.clip(result, min=-bound, max=bound).astype(kind)


def setup_inputs(seed: int = 0) -> dict:
    key_of = jax.random.split(jax.random.key(seed), 11)
    tokens = draw_tokens(jax.random.fold_in(key_of[10], 71), 0)
    segment_ids = jax.vmap(lambda own: jnp.searchsorted(jnp.cumsum(ragged_sizes(own, 4, LEN, LEN // 2, 2)), jnp.arange(LEN), side="right"))(jax.random.split(key_of[1], SEQS_ALL)).reshape((SEQS_ALL, LEN)).astype(jnp.int32)
    qkv_weight = draw_qkv_weight(jax.random.fold_in(key_of[10], 71), 0)
    out_weight = bell_draw(key_of[3], (D, D), (D // 16) ** -0.5, 0.875, ((0, 4), (1, 8)))
    in_weight = bell_draw(key_of[4], (D, FF), D ** -0.5, 0.21875, ((0, 8), (1, 4)))
    down_weight = bell_draw(key_of[5], (FF, D), FF ** -0.5, 0.109375, ((0, 4), (1, 8)))
    qv_bias = bell_draw(key_of[6], (2, N_TENSOR, D // N_TENSOR), 0.5, 3.0, ((1, 4), (2, 8)))
    hidden_bias = bell_draw(key_of[7], (N_TENSOR, FF // N_TENSOR), 0.5, 3.0, ((0, 4), (1, 8)))
    norm_vectors = draw_norm_vectors(jax.random.fold_in(key_of[10], 71), 0)
    cotangent = bell_draw(key_of[9], (SEQS_ALL, LEN, D), 1.0, 6.0, ((0, 8), (1, 4)))
    return dict(tokens=tokens, segment_ids=segment_ids, qkv_weight=qkv_weight, out_weight=out_weight, in_weight=in_weight, down_weight=down_weight, qv_bias=qv_bias, hidden_bias=hidden_bias, norm_vectors=norm_vectors, cotangent=cotangent)


EPS = 1e-05
MASKED = -1e+30

def layer_norm(summed, gain, shift):
    center = summed - lax.optimization_barrier(jnp.mean(summed, -1, keepdims=True))
    inv_std = lax.rsqrt(lax.optimization_barrier(jnp.mean(center * center, -1, keepdims=True)) + EPS)
    normed = center * inv_std
    return (normed * gain + shift, normed, inv_std)

def norm_back(upstream, normed, inv_std, gain):
    scaled = upstream * gain
    return inv_std * (scaled - lax.optimization_barrier(jnp.mean(scaled, -1, keepdims=True)) - normed * lax.optimization_barrier(jnp.mean(scaled * normed, -1, keepdims=True)))

def gelu_parts(inputs):
    cdf_part = 0.5 * (1.0 + lax.erf(inputs * 0.7071067811865476))
    return (inputs * cdf_part, cdf_part + inputs * jnp.exp(-0.5 * inputs * inputs) * 0.3989422804014327)

def rounded_total(partials):
    low = lax.optimization_barrier(partials.astype(jnp.bfloat16))
    return lax.optimization_barrier(jnp.sum(low.astype(jnp.float32), 0))

def group_sum(left, right):
    rows, inner = left.shape
    width = inner // N_TENSOR
    left_groups = left.astype(jnp.float32).reshape(rows, N_TENSOR, width)
    right_groups = right.astype(jnp.float32).reshape(N_TENSOR, width, right.shape[1])
    return rounded_total(jnp.einsum('lgk,gke->gle', left_groups, right_groups))

def reference(tokens, segment_ids, qkv_weight, out_weight, in_weight, down_weight, qv_bias, hidden_bias, norm_vectors, cotangent):
    score_scale = DH ** (-0.5)
    bias_rows = qv_bias.reshape(2, D).astype(jnp.float32)
    hidden_row = hidden_bias.reshape(FF).astype(jnp.float32)
    vector_rows = norm_vectors
    qkv_wide = qkv_weight.astype(jnp.float32)

    def one_sequence(running, inputs):
        seq_tokens, seq_ids, seq_cot = inputs
        projected = jnp.einsum('ld,cde->cle', seq_tokens.astype(jnp.float32), qkv_wide)
        queries = (projected[0] + bias_rows[0]).astype(jnp.bfloat16).reshape(LEN, HEADS, DH)
        key_rows = projected[1].astype(jnp.bfloat16).reshape(LEN, HEADS, DH)
        value_rows = (projected[2] + bias_rows[1]).astype(jnp.bfloat16).reshape(LEN, HEADS, DH)
        scores = jnp.einsum('qhd,khd->hqk', queries.astype(jnp.float32), key_rows.astype(jnp.float32)) * score_scale
        allowed = seq_ids[:, None] == seq_ids[None, :]
        scores = jnp.where(allowed[None], scores, MASKED)
        row_max = lax.optimization_barrier(jnp.max(scores, -1, keepdims=True))
        shifted = jnp.exp(scores - row_max)
        row_total = lax.optimization_barrier(jnp.sum(shifted, -1, keepdims=True))
        log_sum = row_max + jnp.log(row_total)
        attn_probs = (shifted / row_total).astype(jnp.bfloat16)
        context = jnp.einsum('hqk,khd->qhd', attn_probs.astype(jnp.float32), value_rows.astype(jnp.float32)).astype(jnp.bfloat16).reshape(LEN, D)
        attn_out = group_sum(context, out_weight)
        first_sum = seq_tokens.astype(jnp.float32) + attn_out + vector_rows[0]
        normed_one, unit_one, inv_one = layer_norm(first_sum, vector_rows[1], vector_rows[2])
        normed_low = normed_one.astype(jnp.bfloat16)
        hidden_pre = jnp.dot(normed_low, in_weight, preferred_element_type=jnp.float32) + hidden_row
        activated, gelu_slope = gelu_parts(hidden_pre)
        act_low = activated.astype(jnp.bfloat16)
        second_sum = normed_one + group_sum(act_low, down_weight) + vector_rows[3]
        normed_two, unit_two, inv_two = layer_norm(second_sum, vector_rows[4], vector_rows[5])
        layer_out = normed_two.astype(jnp.bfloat16)
        upstream = seq_cot.astype(jnp.float32)
        grad_second = norm_back(upstream, unit_two, inv_two, vector_rows[4])
        second_low = grad_second.astype(jnp.bfloat16)
        down_grad = jnp.dot(act_low.T, second_low, preferred_element_type=jnp.float32)
        grad_hidden = jnp.dot(second_low, down_weight.T, preferred_element_type=jnp.float32) * gelu_slope
        hidden_low = grad_hidden.astype(jnp.bfloat16)
        hidden_grad = lax.optimization_barrier(jnp.sum(grad_hidden, 0))
        in_grad = jnp.dot(normed_low.T, hidden_low, preferred_element_type=jnp.float32)
        grad_normed = grad_second + group_sum(hidden_low, in_weight.T)
        grad_first = norm_back(grad_normed, unit_one, inv_one, vector_rows[1])
        first_low = grad_first.astype(jnp.bfloat16)
        out_grad = jnp.dot(context.T, first_low, preferred_element_type=jnp.float32)
        grad_context = jnp.dot(first_low, out_weight.T, preferred_element_type=jnp.float32).astype(jnp.bfloat16)
        grad_heads = grad_context.reshape(LEN, HEADS, DH).astype(jnp.float32)
        context_heads = context.reshape(LEN, HEADS, DH).astype(jnp.float32)
        row_delta = lax.optimization_barrier(jnp.sum(grad_heads * context_heads, -1))
        probs_again = jnp.exp(scores - log_sum)
        probs_low = probs_again.astype(jnp.bfloat16).astype(jnp.float32)
        value_grad = jnp.einsum('hqk,qhd->khd', probs_low, grad_heads)
        grad_probs = jnp.einsum('qhd,khd->hqk', grad_heads, value_rows.astype(jnp.float32))
        grad_scores = (probs_again * (grad_probs - jnp.transpose(row_delta)[:, :, None])).astype(jnp.bfloat16).astype(jnp.float32)
        query_grad = jnp.einsum('hqk,khd->qhd', grad_scores, key_rows.astype(jnp.float32)) * score_scale
        key_grad = jnp.einsum('hqk,qhd->khd', grad_scores, queries.astype(jnp.float32)) * score_scale
        query_grad = query_grad.reshape(LEN, D)
        key_grad = key_grad.reshape(LEN, D)
        value_grad = value_grad.reshape(LEN, D)
        bias_grad = jnp.stack([lax.optimization_barrier(jnp.sum(query_grad, 0)), lax.optimization_barrier(jnp.sum(value_grad, 0))])
        grads_low = jnp.stack([query_grad, key_grad, value_grad]).astype(jnp.bfloat16)
        qkv_grad = jnp.einsum('ld,cle->cde', seq_tokens.astype(jnp.float32), grads_low.astype(jnp.float32))
        group_width = D // N_TENSOR
        grads_groups = grads_low.astype(jnp.float32).reshape(3, LEN, N_TENSOR, group_width)
        weight_groups = qkv_wide.reshape(3, D, N_TENSOR, group_width)
        token_part = rounded_total(jnp.einsum('clgk,cdgk->gld', grads_groups, weight_groups))
        tokens_grad = (grad_first + token_part).astype(jnp.bfloat16)
        vector_grad = jnp.stack([lax.optimization_barrier(jnp.sum(grad_first, 0)), lax.optimization_barrier(jnp.sum(grad_normed * unit_one, 0)), lax.optimization_barrier(jnp.sum(grad_normed, 0)), lax.optimization_barrier(jnp.sum(grad_second, 0)), lax.optimization_barrier(jnp.sum(upstream * unit_two, 0)), lax.optimization_barrier(jnp.sum(upstream, 0))])
        added = (qkv_grad, out_grad, in_grad, down_grad, bias_grad, hidden_grad, vector_grad)
        running = tuple((total + extra for total, extra in zip(running, added)))
        return (running, (layer_out, tokens_grad))
    start_sums = (jnp.zeros((3, D, D), jnp.float32), jnp.zeros((D, D), jnp.float32), jnp.zeros((D, FF), jnp.float32), jnp.zeros((FF, D), jnp.float32), jnp.zeros((2, D), jnp.float32), jnp.zeros((FF,), jnp.float32), jnp.zeros((6, D), jnp.float32))
    sums, outputs = lax.scan(one_sequence, start_sums, (tokens, segment_ids, cotangent))
    qkv_grad, out_grad, in_grad, down_grad, bias_grad, hidden_grad, vector_grad = sums
    layer_out, tokens_grad = outputs
    return (layer_out, tokens_grad, qkv_grad, out_grad, in_grad, down_grad, bias_grad.reshape(2, N_TENSOR, D // N_TENSOR), hidden_grad.reshape(N_TENSOR, FF // N_TENSOR), vector_grad)
```

```python
import functools
import itertools
import jax
import jax.numpy as jnp
from jax import lax
from jax.experimental import pallas as pl
from jax.experimental.pallas import tpu as pltpu
from jax.sharding import PartitionSpec as P

DH = 64


EPS = 1e-05
MASKED = -1e30
MESH_ID = pl.DeviceIdType.MESH


def remote(src, dst, send_sem, recv_sem, where):
    return pltpu.make_async_remote_copy(
        src_ref=src, dst_ref=dst, send_sem=send_sem, recv_sem=recv_sem,
        device_id=where, device_id_type=MESH_ID)


def line_gather(n, pieces, x, out, send, recv, own):
    me = lax.axis_index("tensor")
    right, left = {"tensor": me + 1}, {"tensor": me - 1}

    def copy(way, step, c, shard, to):
        src = x.at[c] if step == 0 else out.at[shard, c]
        return remote(src, out.at[shard, c], send.at[way, step, c], recv.at[way, step, c], to)

    def landed(way, step, c, shard):
        to = right if way == 0 else left
        remote(out.at[shard, c], out.at[shard, c], send.at[way, step, c], recv.at[way, step, c], to).wait_recv()

    def stage(step):
        if step == 0:
            pltpu.make_async_copy(x, out.at[me], own).start()
        for c in range(pieces):
            if step > 0:
                pl.when(me - step >= 0)(lambda: landed(0, step - 1, c, me - step))
                pl.when(me + step <= n - 1)(lambda: landed(1, step - 1, c, me + step))
            if step < n - 1:
                pl.when((me < n - 1) & (me - step >= 0))(lambda: copy(0, step, c, me - step, right).start())
                pl.when((me > 0) & (me + step <= n - 1))(lambda: copy(1, step, c, me + step, left).start())

    def finish():
        pltpu.make_async_copy(x, out.at[me], own).wait()
        for step in range(n - 1):
            for c in range(pieces):
                pl.when((me < n - 1) & (me - step >= 0))(lambda: copy(0, step, c, me - step, right).wait_send())
                pl.when((me > 0) & (me + step <= n - 1))(lambda: copy(1, step, c, me + step, left).wait_send())

    return [functools.partial(stage, s) for s in range(n)] + [finish]


def line_scatter(n, pieces, p, out, got, acc, send, recv):
    me = lax.axis_index("tensor")
    right, left = {"tensor": me + 1}, {"tensor": me - 1}

    def copy(way, t, c):
        return remote(acc.at[way, t, c], got.at[way, t, c], send.at[way, t, c], recv.at[way, t, c],
                      right if way == 0 else left)

    def push(way, t, c, d):
        first = me == 0 if way == 0 else me == n - 1

        @pl.when(first)
        def _():
            acc[way, t, c] = p[d, c]

        @pl.when(jnp.logical_not(first))
        def _():
            copy(way, t, c).wait_recv()
            acc[way, t, c] = (p[d, c].astype(jnp.float32) + got[way, t, c].astype(jnp.float32)).astype(acc.dtype)

        copy(way, t, c).start()

    def stage(t):
        for c in range(pieces):
            pl.when(n - 1 - t > me)(lambda: push(0, t, c, n - 1 - t))
            pl.when(t < me)(lambda: push(1, t, c, t))

    def take(way, t, c):
        copy(way, t, c).wait_recv()
        out[c] += got[way, t, c].astype(jnp.float32)

    def finish():
        for c in range(pieces):
            out[c] = p[me, c].astype(jnp.float32)
        for t in range(n - 1):
            for c in range(pieces):
                pl.when((me > 0) & (n - 1 - t == me))(lambda: take(0, t, c))
                pl.when((me < n - 1) & (t == me))(lambda: take(1, t, c))
        for t in range(n - 1):
            for c in range(pieces):
                pl.when(n - 1 - t > me)(lambda: copy(0, t, c).wait_send())
                pl.when(t < me)(lambda: copy(1, t, c).wait_send())

    return [functools.partial(stage, t) for t in range(n - 1)] + [finish]


def pair_place(n):
    me = lax.axis_index("dp")
    core = lax.rem(me, 2)
    chip = (me - core) // 2
    twin = {"dp": me + 1 - 2 * core}
    return me, core, chip, twin


def group_gather(n, x, out, send, recv, fsend, frecv, own):
    me, core, chip, twin = pair_place(n)
    chips = n // 2

    def far(j):
        to = lax.rem(chip + j, chips) * 2 + core
        return remote(x, out.at[me], send.at[j], recv.at[j], {"dp": to})

    def source(j):
        return lax.rem(chip - j + chips, chips) * 2 + core

    def near(j):
        at = source(j)
        return remote(x if j == 0 else out.at[at], out.at[at], fsend.at[j], frecv.at[j], twin)

    def landed(j, at, sem_s, sem_r):
        remote(out.at[at], out.at[at], sem_s.at[j], sem_r.at[j], twin).wait_recv()

    def begin():
        for j in range(1, chips):
            far(j).start()
        near(0).start()
        pltpu.make_async_copy(x, out.at[me], own).start()

    def relay():
        for j in range(1, chips):
            landed(j, source(j), send, recv)
            near(j).start()

    def finish():
        for j in range(chips):
            landed(j, source(j) + 1 - 2 * core, fsend, frecv)
            near(j).wait_send()
        for j in range(1, chips):
            far(j).wait_send()
        pltpu.make_async_copy(x, out.at[me], own).wait()

    return [begin, relay, finish]


def group_scatter(n, g, out, tgot, both, fgot, send, recv, fsend, frecv):
    me, core, chip, twin = pair_place(n)
    chips = n // 2

    def near(j):
        to = lax.rem(chip + j, chips)
        return remote(g.at[to * 2 + 1 - core], tgot.at[j], fsend.at[j], frecv.at[j], twin)

    def far(j):
        to = lax.rem(chip + j, chips) * 2 + core
        return remote(both.at[j], fgot.at[j], send.at[j], recv.at[j], {"dp": to})

    order = list(range(1, chips)) + [0]

    def begin():
        for j in order:
            near(j).start()

    def spread():
        for j in order:
            near(j).wait_recv()
            mine = lax.rem(chip + j, chips) * 2 + core
            total = g[mine].astype(jnp.float32) + tgot[j].astype(jnp.float32)
            if j == 0:
                out[...] = total
            else:
                both[j] = total.astype(both.dtype)
                far(j).start()

    def finish():
        for j in range(1, chips):
            far(j).wait_recv()
            out[...] += fgot[j].astype(jnp.float32)
        for j in range(chips):
            near(j).wait_send()
        for j in range(1, chips):
            far(j).wait_send()

    return [begin, spread, finish]


def exchange(mesh, ident, gather=(), scatter=(), wide_gather=(), wide_scatter=()):
    n, m = mesh.shape["tensor"], mesh.shape["dp"]
    dma = pltpu.SemaphoreType.DMA
    vmem = pl.BlockSpec(memory_space=pltpu.VMEM)
    outs, specs, scratch, groups = [], [], [], []
    for x in gather:
        outs.append(jax.ShapeDtypeStruct((n,) + x.shape, x.dtype))
        specs.append(pl.BlockSpec(memory_space=pl.ANY))
        own = [dma((2, n - 1, x.shape[0])), dma((2, n - 1, x.shape[0])), dma]
        groups.append((functools.partial(line_gather, n, x.shape[0]), len(own)))
        scratch += own
    for x in scatter:
        outs.append(jax.ShapeDtypeStruct(x.shape[1:], jnp.float32))
        specs.append(vmem)
        slots = (2, n - 1) + x.shape[1:]
        own = [pltpu.VMEM(slots, x.dtype)] * 2 + [dma((2, n - 1, x.shape[1]))] * 2
        groups.append((functools.partial(line_scatter, n, x.shape[1]), len(own)))
        scratch += own
    for x in wide_gather:
        outs.append(jax.ShapeDtypeStruct((m,) + x.shape, x.dtype))
        specs.append(pl.BlockSpec(memory_space=pl.ANY))
        own = [dma((m // 2,))] * 4 + [dma]
        groups.append((functools.partial(group_gather, m), len(own)))
        scratch += own
    for x in wide_scatter:
        outs.append(jax.ShapeDtypeStruct(x.shape[1:], jnp.float32))
        specs.append(vmem)
        own = [pltpu.VMEM((m // 2,) + x.shape[1:], x.dtype)] * 3 + [dma((m // 2,))] * 4
        groups.append((functools.partial(group_scatter, m), len(own)))
        scratch += own
    operands = list(gather) + list(scatter) + list(wide_gather) + list(wide_scatter)
    count = len(operands)

    def kernel(*refs):
        ins, results, rest = refs[:count], refs[count:2 * count], list(refs[2 * count:])
        barrier = pltpu.get_barrier_semaphore()
        me = lax.axis_index("tensor")

        def greet(where):
            pl.semaphore_signal(barrier, inc=1, device_id=where, device_id_type=MESH_ID)

        if gather or scatter:
            pl.when(me > 0)(lambda: greet({"tensor": me - 1}))
            pl.when(me < n - 1)(lambda: greet({"tensor": me + 1}))
        if wide_gather or wide_scatter:
            _, core, chip, twin = pair_place(m)
            greet(twin)
            for j in range(1, m // 2):
                greet({"dp": lax.rem(chip + j, m // 2) * 2 + core})
        peers = m // 2 if wide_gather or wide_scatter else 0
        if gather or scatter:
            peers = peers + (me > 0).astype(jnp.int32) + (me < n - 1).astype(jnp.int32)
        pl.semaphore_wait(barrier, peers)
        plans = []
        for i, (make, size) in enumerate(groups):
            own, rest = rest[:size], rest[size:]
            plans.append(make(ins[i], results[i], *own))
        plans = plans[::-1]
        for row in itertools.zip_longest(*plans):
            for stage in row:
                if stage is not None:
                    stage()

    return pl.pallas_call(
        kernel, out_shape=tuple(outs), in_specs=[vmem] * count, out_specs=tuple(specs),
        scratch_shapes=scratch, name=f"exchange_{ident}",
        compiler_params=pltpu.CompilerParams(
            collective_id=ident, has_side_effects=True, vmem_limit_bytes=48 * 1024 * 1024),
    )(*operands)


PIECES = 2

def layer_norm(summed, gain, shift):
    center = summed - jnp.mean(summed, -1, keepdims=True)
    inv_std = lax.rsqrt(jnp.mean(center * center, -1, keepdims=True) + EPS)
    normed = center * inv_std
    return (normed * gain + shift, normed, inv_std)


def norm_back(upstream, normed, inv_std, gain):
    scaled = upstream * gain
    return inv_std * (
        scaled
        - jnp.mean(scaled, -1, keepdims=True)
        - normed * jnp.mean(scaled * normed, -1, keepdims=True)
    )


def gelu_parts(inputs):
    cdf_part = 0.5 * (1.0 + lax.erf(inputs * 0.7071067811865476))
    return (
        inputs * cdf_part,
        cdf_part + inputs * jnp.exp(-0.5 * inputs * inputs) * 0.3989422804014327,
    )


def local(
    mesh,
    tokens,
    segment_ids,
    qkv_weight,
    out_weight,
    in_weight,
    down_weight,
    qv_bias,
    hidden_bias,
    norm_vectors,
    cotangent,
):
    n, m = mesh.shape["tensor"], mesh.shape["dp"]
    seq_count, rows, width = tokens.shape
    share = qkv_weight.shape[1]
    part = qkv_weight.shape[2]
    hidden = in_weight.shape[1]
    qkv_cols = 3 * part
    marks = (qkv_cols, qkv_cols + part, qkv_cols + part + hidden)
    packed = jnp.concatenate(
        [qkv_weight[0], qkv_weight[1], qkv_weight[2], out_weight.T, in_weight, down_weight.T], axis=1
    )
    bias_len, hid_len = qv_bias.shape[2], hidden_bias.shape[1]
    vec_len = norm_vectors.shape[1]
    small = jnp.concatenate(
        [qv_bias.astype(jnp.float32).reshape(-1), hidden_bias.astype(jnp.float32).reshape(-1), norm_vectors.reshape(-1)]
    )
    small_len = small.shape[0]
    tile = -(-small_len // 1024) * 8
    small = jnp.pad(small, (0, tile * 128 - small_len)).reshape(tile, 128)

    def pieces_of(rows_in):
        return rows_in.reshape(PIECES, -1, width)

    def split(part_rows):
        return part_rows.astype(jnp.bfloat16).reshape(n, PIECES, -1, width)

    def whole(gathered):
        return gathered.reshape(seq_count, -1, width)

    tokens_all, packed_all, small_all = exchange(
        mesh, 1, gather=(pieces_of(tokens),), wide_gather=(packed, small)
    )
    full_tokens = whole(tokens_all)
    weights = packed_all.reshape(m * share, -1)
    qkv_full = weights[:, : marks[0]]
    out_full, in_full, down_full = (
        weights[:, marks[0] : marks[1]],
        weights[:, marks[1] : marks[2]],
        weights[:, marks[2] :],
    )
    small_all = small_all.reshape(m, -1)
    qv_full = small_all[:, : 2 * bias_len].reshape(m, 2, bias_len).transpose(1, 0, 2).reshape(2, -1)
    hidden_full = small_all[:, 2 * bias_len : 2 * bias_len + hid_len].reshape(-1)
    norm_here = small_all.reshape(1, -1, 128)
    length = full_tokens.shape[1]
    local_width = part
    heads_here = local_width // DH
    score_scale = DH ** (-0.5)
    block_rows = min(512, length)
    block_count = length // block_rows
    head_shape = (seq_count, length, heads_here, DH)
    flat = jnp.einsum("bld,de->ble", full_tokens, qkv_full, preferred_element_type=jnp.float32)
    projected = [flat[..., c * part : (c + 1) * part] for c in range(3)]
    queries = (projected[0] + qv_full[0]).astype(jnp.bfloat16).reshape(head_shape)
    key_rows = projected[1].astype(jnp.bfloat16).reshape(head_shape)
    value_rows = (projected[2] + qv_full[1]).astype(jnp.bfloat16).reshape(head_shape)

    def block_scores(block_index):
        row_start = block_index * block_rows
        query_block = lax.dynamic_slice_in_dim(queries, row_start, block_rows, 1)
        segment_block = lax.dynamic_slice_in_dim(segment_ids, row_start, block_rows, 1)
        scores = (
            jnp.einsum("bqhd,bkhd->bhqk", query_block, key_rows, preferred_element_type=jnp.float32)
            * score_scale
        )
        allowed = segment_block[:, None, :, None] == segment_ids[:, None, None, :]
        return (jnp.where(allowed, scores, MASKED), query_block)

    def attend(block_index):
        scores, query_block = block_scores(block_index)
        row_max = jnp.max(scores, -1, keepdims=True)
        shifted = jnp.exp(scores - row_max)
        row_total = jnp.sum(shifted, -1, keepdims=True)
        attn_probs = (shifted / row_total).astype(jnp.bfloat16)
        context = jnp.einsum(
            "bhqk,bkhd->bqhd", attn_probs, value_rows, preferred_element_type=jnp.float32
        ).astype(jnp.bfloat16)
        return (context, (row_max + jnp.log(row_total))[..., 0])

    contexts, log_sums = lax.map(attend, jnp.arange(block_count))
    context_rows = jnp.moveaxis(contexts, 0, 1).reshape(seq_count, length, local_width)
    attn_part = jnp.einsum(
        "ble,de->bld", context_rows, out_full, preferred_element_type=jnp.float32
    )
    norm_all, attn_sum = exchange(mesh, 2, gather=(norm_here,), scatter=(split(attn_part),))
    attn_sum = attn_sum.reshape(tokens.shape)
    norm_all = norm_all.reshape(n, m, -1)[:, :, 2 * bias_len + hid_len : small_len]
    vector_rows = norm_all.reshape(n, m, 6, vec_len).transpose(2, 1, 0, 3).reshape(6, -1)
    first_sum = tokens.astype(jnp.float32) + attn_sum + vector_rows[0]
    normed_one, unit_one, inv_one = layer_norm(first_sum, vector_rows[1], vector_rows[2])
    (normed_all,) = exchange(mesh, 3, gather=(pieces_of(normed_one.astype(jnp.bfloat16)),))
    normed_full = whole(normed_all)
    hidden_pre = (
        jnp.einsum("bld,df->blf", normed_full, in_full, preferred_element_type=jnp.float32)
        + hidden_full
    )
    activated, gelu_slope = gelu_parts(hidden_pre)
    act_low = activated.astype(jnp.bfloat16)
    mlp_part = jnp.einsum("blf,df->bld", act_low, down_full, preferred_element_type=jnp.float32)
    (mlp_sum,) = exchange(mesh, 4, scatter=(split(mlp_part),))
    mlp_sum = mlp_sum.reshape(tokens.shape)
    second_sum = normed_one + mlp_sum + vector_rows[3]
    normed_two, unit_two, inv_two = layer_norm(second_sum, vector_rows[4], vector_rows[5])
    layer_out = normed_two.astype(jnp.bfloat16)
    upstream = cotangent.astype(jnp.float32)
    grad_second = norm_back(upstream, unit_two, inv_two, vector_rows[4])
    (grad_mlp_all,) = exchange(mesh, 3, gather=(pieces_of(grad_second.astype(jnp.bfloat16)),))
    grad_mlp_full = whole(grad_mlp_all)
    down_grad = jnp.einsum(
        "bld,blf->df", grad_mlp_full, act_low, preferred_element_type=jnp.float32
    )
    grad_hidden = (
        jnp.einsum("bld,df->blf", grad_mlp_full, down_full, preferred_element_type=jnp.float32)
        * gelu_slope
    )
    hidden_low = grad_hidden.astype(jnp.bfloat16)
    hidden_grad = jnp.sum(grad_hidden, (0, 1))[None]
    in_grad = jnp.einsum("bld,blf->df", normed_full, hidden_low, preferred_element_type=jnp.float32)
    back_part = jnp.einsum("blf,df->bld", hidden_low, in_full, preferred_element_type=jnp.float32)
    (back_sum,) = exchange(mesh, 4, scatter=(split(back_part),))
    grad_normed = grad_second + back_sum.reshape(tokens.shape)
    grad_first = norm_back(grad_normed, unit_one, inv_one, vector_rows[1])
    vector_grad = jnp.stack(
        [
            jnp.sum(grad_first, (0, 1)),
            jnp.sum(grad_normed * unit_one, (0, 1)),
            jnp.sum(grad_normed, (0, 1)),
            jnp.sum(grad_second, (0, 1)),
            jnp.sum(upstream * unit_two, (0, 1)),
            jnp.sum(upstream, (0, 1)),
        ]
    )
    vector_tile = jnp.pad(vector_grad, ((0, 2), (0, 0)))[None]
    grad_attn_all, vector_all = exchange(
        mesh, 5, gather=(pieces_of(grad_first.astype(jnp.bfloat16)), vector_tile)
    )
    grad_attn_full = whole(grad_attn_all)
    vector_sum = jnp.sum(vector_all[:, 0, :6], 0).reshape(6, m, n, vec_len)
    vector_here = lax.dynamic_index_in_dim(vector_sum, lax.axis_index("tensor"), 2, keepdims=False)
    out_grad = jnp.einsum(
        "bld,ble->de", grad_attn_full, context_rows, preferred_element_type=jnp.float32
    )
    grad_context = jnp.einsum(
        "bld,de->ble", grad_attn_full, out_full, preferred_element_type=jnp.float32
    ).astype(jnp.bfloat16)
    grad_heads = grad_context.reshape(head_shape)
    row_delta = jnp.sum(
        grad_heads.astype(jnp.float32) * context_rows.reshape(head_shape).astype(jnp.float32), -1
    )

    def backward_block(running, block_index):
        key_grad, value_grad = running
        scores, query_block = block_scores(block_index)
        row_start = block_index * block_rows
        grad_block = lax.dynamic_slice_in_dim(grad_heads, row_start, block_rows, 1)
        delta_block = lax.dynamic_slice_in_dim(row_delta, row_start, block_rows, 1)
        probs_again = jnp.exp(scores - log_sums[block_index][..., None])
        probs_low = probs_again.astype(jnp.bfloat16)
        value_grad = value_grad + jnp.einsum(
            "bhqk,bqhd->bkhd", probs_low, grad_block, preferred_element_type=jnp.float32
        )
        grad_probs = jnp.einsum(
            "bqhd,bkhd->bhqk", grad_block, value_rows, preferred_element_type=jnp.float32
        )
        grad_scores = (
            probs_again * (grad_probs - jnp.transpose(delta_block, (0, 2, 1))[..., None])
        ).astype(jnp.bfloat16)
        query_grad = (
            jnp.einsum("bhqk,bkhd->bqhd", grad_scores, key_rows, preferred_element_type=jnp.float32)
            * score_scale
        )
        key_grad = (
            key_grad
            + jnp.einsum(
                "bhqk,bqhd->bkhd", grad_scores, query_block, preferred_element_type=jnp.float32
            )
            * score_scale
        )
        return ((key_grad, value_grad), query_grad)

    zero_heads = jnp.zeros(head_shape, jnp.float32)
    (key_grad, value_grad), query_grads = lax.scan(
        backward_block, (zero_heads, zero_heads), jnp.arange(block_count)
    )
    query_grad = jnp.moveaxis(query_grads, 0, 1).reshape(seq_count, length, local_width)
    key_grad = key_grad.reshape(seq_count, length, local_width)
    value_grad = value_grad.reshape(seq_count, length, local_width)
    bias_grad = jnp.stack([jnp.sum(query_grad, (0, 1)), jnp.sum(value_grad, (0, 1))])
    grads_low = jnp.concatenate([query_grad, key_grad, value_grad], -1).astype(jnp.bfloat16)
    qkv_grad = jnp.einsum("bld,ble->de", full_tokens, grads_low, preferred_element_type=jnp.float32)
    token_part = jnp.einsum("ble,de->bld", grads_low, qkv_full, preferred_element_type=jnp.float32)
    grads = jnp.concatenate(
        [g.astype(jnp.bfloat16) for g in (qkv_grad, out_grad, in_grad, down_grad)], axis=1
    ).reshape(m, share, -1)
    small_grads = jnp.concatenate(
        [
            bias_grad.reshape(2, m, bias_len).transpose(1, 0, 2).reshape(m, -1),
            hidden_grad.reshape(m, hid_len),
            vector_here.transpose(1, 0, 2).reshape(m, -1),
        ],
        axis=1,
    )
    small_grads = jnp.pad(small_grads, ((0, 0), (0, tile * 128 - small_len))).reshape(m, tile, 128)
    token_sum, grad_sum, small_sum = exchange(
        mesh, 6, scatter=(split(token_part),), wide_scatter=(grads, small_grads)
    )
    tokens_grad = (grad_first + token_sum.reshape(tokens.shape)).astype(jnp.bfloat16)
    qkv_shard = jnp.stack([grad_sum[:, c * part : (c + 1) * part] for c in range(3)])
    out_shard = grad_sum[:, marks[0] : marks[1]].T
    in_shard = grad_sum[:, marks[1] : marks[2]]
    down_shard = grad_sum[:, marks[2] :].T
    small_sum = small_sum.reshape(-1)
    bias_shard = small_sum[: 2 * bias_len].reshape(qv_bias.shape)
    hidden_shard = small_sum[2 * bias_len : 2 * bias_len + hid_len].reshape(hidden_bias.shape)
    vectors_grad = small_sum[2 * bias_len + hid_len : small_len].reshape(norm_vectors.shape)
    return (
        layer_out,
        tokens_grad,
        qkv_shard,
        out_shard,
        in_shard,
        down_shard,
        bias_shard,
        hidden_shard,
        vectors_grad,
    )


def solution(mesh):
    return jax.shard_map(
        functools.partial(local, mesh),
        mesh=mesh,
        in_specs=(
            P("dp", "tensor", None),
            P("dp", None),
            P(None, "dp", "tensor"),
            P("tensor", "dp"),
            P("dp", "tensor"),
            P("tensor", "dp"),
            P(None, "tensor", "dp"),
            P("tensor", "dp"),
            P(None, ("dp", "tensor")),
            P("dp", "tensor", None),
        ),
        out_specs=(
            P("dp", "tensor", None),
            P("dp", "tensor", None),
            P(None, "dp", "tensor"),
            P("tensor", "dp"),
            P("dp", "tensor"),
            P("tensor", "dp"),
            P(None, "tensor", "dp"),
            P("tensor", "dp"),
            P(None, ("dp", "tensor")),
        ),
        check_vma=False,
    )
```

```python
import functools
import itertools
import jax
import jax.numpy as jnp
from jax import lax
from jax.experimental import pallas as pl
from jax.experimental.pallas import tpu as pltpu
from jax.sharding import PartitionSpec as P

DH = 64


EPS = 1e-05
MASKED = -1e30
MESH_ID = pl.DeviceIdType.MESH


def remote(src, dst, send_sem, recv_sem, where):
    return pltpu.make_async_remote_copy(
        src_ref=src, dst_ref=dst, send_sem=send_sem, recv_sem=recv_sem,
        device_id=where, device_id_type=MESH_ID)


def line_gather(n, pieces, x, out, send, recv, own):
    me = lax.axis_index("tensor")
    right, left = {"tensor": me + 1}, {"tensor": me - 1}

    def copy(way, step, c, shard, to):
        src = x.at[c] if step == 0 else out.at[shard, c]
        return remote(src, out.at[shard, c], send.at[way, step, c], recv.at[way, step, c], to)

    def landed(way, step, c, shard):
        to = right if way == 0 else left
        remote(out.at[shard, c], out.at[shard, c], send.at[way, step, c], recv.at[way, step, c], to).wait_recv()

    def stage(step):
        if step == 0:
            pltpu.make_async_copy(x, out.at[me], own).start()
        for c in range(pieces):
            if step > 0:
                pl.when(me - step >= 0)(lambda: landed(0, step - 1, c, me - step))
                pl.when(me + step <= n - 1)(lambda: landed(1, step - 1, c, me + step))
            if step < n - 1:
                pl.when((me < n - 1) & (me - step >= 0))(lambda: copy(0, step, c, me - step, right).start())
                pl.when((me > 0) & (me + step <= n - 1))(lambda: copy(1, step, c, me + step, left).start())

    def finish():
        pltpu.make_async_copy(x, out.at[me], own).wait()
        for step in range(n - 1):
            for c in range(pieces):
                pl.when((me < n - 1) & (me - step >= 0))(lambda: copy(0, step, c, me - step, right).wait_send())
                pl.when((me > 0) & (me + step <= n - 1))(lambda: copy(1, step, c, me + step, left).wait_send())

    return [functools.partial(stage, s) for s in range(n)] + [finish]


def line_scatter(n, pieces, p, out, got, acc, send, recv):
    me = lax.axis_index("tensor")
    right, left = {"tensor": me + 1}, {"tensor": me - 1}

    def copy(way, t, c):
        return remote(acc.at[way, t, c], got.at[way, t, c], send.at[way, t, c], recv.at[way, t, c],
                      right if way == 0 else left)

    def push(way, t, c, d):
        first = me == 0 if way == 0 else me == n - 1

        @pl.when(first)
        def _():
            acc[way, t, c] = p[d, c]

        @pl.when(jnp.logical_not(first))
        def _():
            copy(way, t, c).wait_recv()
            acc[way, t, c] = (p[d, c].astype(jnp.float32) + got[way, t, c].astype(jnp.float32)).astype(acc.dtype)

        copy(way, t, c).start()

    def stage(t):
        for c in range(pieces):
            pl.when(n - 1 - t > me)(lambda: push(0, t, c, n - 1 - t))
            pl.when(t < me)(lambda: push(1, t, c, t))

    def take(way, t, c):
        copy(way, t, c).wait_recv()
        out[c] += got[way, t, c].astype(jnp.float32)

    def finish():
        for c in range(pieces):
            out[c] = p[me, c].astype(jnp.float32)
        for t in range(n - 1):
            for c in range(pieces):
                pl.when((me > 0) & (n - 1 - t == me))(lambda: take(0, t, c))
                pl.when((me < n - 1) & (t == me))(lambda: take(1, t, c))
        for t in range(n - 1):
            for c in range(pieces):
                pl.when(n - 1 - t > me)(lambda: copy(0, t, c).wait_send())
                pl.when(t < me)(lambda: copy(1, t, c).wait_send())

    return [functools.partial(stage, t) for t in range(n - 1)] + [finish]


def pair_place(n):
    me = lax.axis_index("dp")
    core = lax.rem(me, 2)
    chip = (me - core) // 2
    twin = {"dp": me + 1 - 2 * core}
    return me, core, chip, twin


def group_gather(n, x, out, send, recv, fsend, frecv, own):
    me, core, chip, twin = pair_place(n)
    chips = n // 2

    def far(j):
        to = lax.rem(chip + j, chips) * 2 + core
        return remote(x, out.at[me], send.at[j], recv.at[j], {"dp": to})

    def source(j):
        return lax.rem(chip - j + chips, chips) * 2 + core

    def near(j):
        at = source(j)
        return remote(x if j == 0 else out.at[at], out.at[at], fsend.at[j], frecv.at[j], twin)

    def landed(j, at, sem_s, sem_r):
        remote(out.at[at], out.at[at], sem_s.at[j], sem_r.at[j], twin).wait_recv()

    def begin():
        for j in range(1, chips):
            far(j).start()
        near(0).start()
        pltpu.make_async_copy(x, out.at[me], own).start()

    def relay():
        for j in range(1, chips):
            landed(j, source(j), send, recv)
            near(j).start()

    def finish():
        for j in range(chips):
            landed(j, source(j) + 1 - 2 * core, fsend, frecv)
            near(j).wait_send()
        for j in range(1, chips):
            far(j).wait_send()
        pltpu.make_async_copy(x, out.at[me], own).wait()

    return [begin, relay, finish]


def group_scatter(n, g, out, tgot, both, fgot, send, recv, fsend, frecv):
    me, core, chip, twin = pair_place(n)
    chips = n // 2

    def near(j):
        to = lax.rem(chip + j, chips)
        return remote(g.at[to * 2 + 1 - core], tgot.at[j], fsend.at[j], frecv.at[j], twin)

    def far(j):
        to = lax.rem(chip + j, chips) * 2 + core
        return remote(both.at[j], fgot.at[j], send.at[j], recv.at[j], {"dp": to})

    order = list(range(1, chips)) + [0]

    def begin():
        for j in order:
            near(j).start()

    def spread():
        for j in order:
            near(j).wait_recv()
            mine = lax.rem(chip + j, chips) * 2 + core
            total = g[mine].astype(jnp.float32) + tgot[j].astype(jnp.float32)
            if j == 0:
                out[...] = total
            else:
                both[j] = total.astype(both.dtype)
                far(j).start()

    def finish():
        for j in range(1, chips):
            far(j).wait_recv()
            out[...] += fgot[j].astype(jnp.float32)
        for j in range(chips):
            near(j).wait_send()
        for j in range(1, chips):
            far(j).wait_send()

    return [begin, spread, finish]


def exchange(mesh, ident, gather=(), scatter=(), wide_gather=(), wide_scatter=()):
    n, m = mesh.shape["tensor"], mesh.shape["dp"]
    dma = pltpu.SemaphoreType.DMA
    vmem = pl.BlockSpec(memory_space=pltpu.VMEM)
    outs, specs, scratch, groups = [], [], [], []
    for x in gather:
        outs.append(jax.ShapeDtypeStruct((n,) + x.shape, x.dtype))
        specs.append(pl.BlockSpec(memory_space=pl.ANY))
        own = [dma((2, n - 1, x.shape[0])), dma((2, n - 1, x.shape[0])), dma]
        groups.append((functools.partial(line_gather, n, x.shape[0]), len(own)))
        scratch += own
    for x in scatter:
        outs.append(jax.ShapeDtypeStruct(x.shape[1:], jnp.float32))
        specs.append(vmem)
        slots = (2, n - 1) + x.shape[1:]
        own = [pltpu.VMEM(slots, x.dtype)] * 2 + [dma((2, n - 1, x.shape[1]))] * 2
        groups.append((functools.partial(line_scatter, n, x.shape[1]), len(own)))
        scratch += own
    for x in wide_gather:
        outs.append(jax.ShapeDtypeStruct((m,) + x.shape, x.dtype))
        specs.append(pl.BlockSpec(memory_space=pl.ANY))
        own = [dma((m // 2,))] * 4 + [dma]
        groups.append((functools.partial(group_gather, m), len(own)))
        scratch += own
    for x in wide_scatter:
        outs.append(jax.ShapeDtypeStruct(x.shape[1:], jnp.float32))
        specs.append(vmem)
        own = [pltpu.VMEM((m // 2,) + x.shape[1:], x.dtype)] * 3 + [dma((m // 2,))] * 4
        groups.append((functools.partial(group_scatter, m), len(own)))
        scratch += own
    operands = list(gather) + list(scatter) + list(wide_gather) + list(wide_scatter)
    count = len(operands)

    def kernel(*refs):
        ins, results, rest = refs[:count], refs[count:2 * count], list(refs[2 * count:])
        barrier = pltpu.get_barrier_semaphore()
        me = lax.axis_index("tensor")

        def greet(where):
            pl.semaphore_signal(barrier, inc=1, device_id=where, device_id_type=MESH_ID)

        if gather or scatter:
            pl.when(me > 0)(lambda: greet({"tensor": me - 1}))
            pl.when(me < n - 1)(lambda: greet({"tensor": me + 1}))
        if wide_gather or wide_scatter:
            _, core, chip, twin = pair_place(m)
            greet(twin)
            for j in range(1, m // 2):
                greet({"dp": lax.rem(chip + j, m // 2) * 2 + core})
        peers = m // 2 if wide_gather or wide_scatter else 0
        if gather or scatter:
            peers = peers + (me > 0).astype(jnp.int32) + (me < n - 1).astype(jnp.int32)
        pl.semaphore_wait(barrier, peers)
        plans = []
        for i, (make, size) in enumerate(groups):
            own, rest = rest[:size], rest[size:]
            plans.append(make(ins[i], results[i], *own))
        lines = plans[: len(gather) + len(scatter)][::-1]
        wides = plans[len(lines) :][::-1]
        run_stage = [lambda p=p: p[0]() for p in wides] + [lambda p=p: p[0]() for p in lines]
        middle = [p[1] for p in wides]
        along = [stage for row in itertools.zip_longest(*[p[1:-1] for p in lines]) for stage in row if stage]
        run_stage += along[:-1] + middle + along[-1:] if wide_gather else middle + along
        run_stage += [p[-1] for p in lines] + [p[-1] for p in wides]
        for stage in run_stage:
            stage()

    return pl.pallas_call(
        kernel, out_shape=tuple(outs), in_specs=[vmem] * count, out_specs=tuple(specs),
        scratch_shapes=scratch, name=f"exchange_{ident}",
        compiler_params=pltpu.CompilerParams(
            collective_id=ident, has_side_effects=True, vmem_limit_bytes=48 * 1024 * 1024),
    )(*operands)


PIECES = 2

def layer_norm(summed, gain, shift):
    center = summed - jnp.mean(summed, -1, keepdims=True)
    inv_std = lax.rsqrt(jnp.mean(center * center, -1, keepdims=True) + EPS)
    normed = center * inv_std
    return (normed * gain + shift, normed, inv_std)


def norm_back(upstream, normed, inv_std, gain):
    scaled = upstream * gain
    return inv_std * (
        scaled
        - jnp.mean(scaled, -1, keepdims=True)
        - normed * jnp.mean(scaled * normed, -1, keepdims=True)
    )


def gelu_parts(inputs):
    cdf_part = 0.5 * (1.0 + lax.erf(inputs * 0.7071067811865476))
    return (
        inputs * cdf_part,
        cdf_part + inputs * jnp.exp(-0.5 * inputs * inputs) * 0.3989422804014327,
    )


def local(
    mesh,
    tokens,
    segment_ids,
    qkv_weight,
    out_weight,
    in_weight,
    down_weight,
    qv_bias,
    hidden_bias,
    norm_vectors,
    cotangent,
):
    n, m = mesh.shape["tensor"], mesh.shape["dp"]
    seq_count, rows, width = tokens.shape
    share = qkv_weight.shape[1]
    part = qkv_weight.shape[2]
    hidden = in_weight.shape[1]
    qkv_cols = 3 * part
    marks = (qkv_cols, qkv_cols + part, qkv_cols + part + hidden)
    packed = jnp.concatenate(
        [qkv_weight[0], qkv_weight[1], qkv_weight[2], out_weight.T, in_weight, down_weight.T], axis=1
    )
    bias_len, hid_len = qv_bias.shape[2], hidden_bias.shape[1]
    vec_len = norm_vectors.shape[1]
    small = jnp.concatenate(
        [qv_bias.astype(jnp.float32).reshape(-1), hidden_bias.astype(jnp.float32).reshape(-1), norm_vectors.reshape(-1)]
    )
    small_len = small.shape[0]
    tile = -(-small_len // 1024) * 8
    small = jnp.pad(small, (0, tile * 128 - small_len)).reshape(tile, 128)

    def pieces_of(rows_in):
        return rows_in.reshape(PIECES, -1, width)

    def split(part_rows):
        return part_rows.astype(jnp.bfloat16).reshape(n, PIECES, -1, width)

    def whole(gathered):
        return gathered.reshape(seq_count, -1, width)

    tokens_all, packed_all, small_all = exchange(
        mesh, 1, gather=(pieces_of(tokens),), wide_gather=(packed, small)
    )
    full_tokens = whole(tokens_all)
    weights = packed_all.reshape(m * share, -1)
    qkv_full = weights[:, : marks[0]]
    out_full, in_full, down_full = (
        weights[:, marks[0] : marks[1]],
        weights[:, marks[1] : marks[2]],
        weights[:, marks[2] :],
    )
    small_all = small_all.reshape(m, -1)
    qv_full = small_all[:, : 2 * bias_len].reshape(m, 2, bias_len).transpose(1, 0, 2).reshape(2, -1)
    hidden_full = small_all[:, 2 * bias_len : 2 * bias_len + hid_len].reshape(-1)
    norm_here = small_all.reshape(1, -1, 128)
    length = full_tokens.shape[1]
    local_width = part
    heads_here = local_width // DH
    score_scale = DH ** (-0.5)
    block_rows = min(512, length)
    block_count = length // block_rows
    head_shape = (seq_count, length, heads_here, DH)
    flat = jnp.einsum("bld,de->ble", full_tokens, qkv_full, preferred_element_type=jnp.float32)
    projected = [flat[..., c * part : (c + 1) * part] for c in range(3)]
    queries = (projected[0] + qv_full[0]).astype(jnp.bfloat16).reshape(head_shape)
    key_rows = projected[1].astype(jnp.bfloat16).reshape(head_shape)
    value_rows = (projected[2] + qv_full[1]).astype(jnp.bfloat16).reshape(head_shape)

    def block_scores(block_index):
        row_start = block_index * block_rows
        query_block = lax.dynamic_slice_in_dim(queries, row_start, block_rows, 1)
        segment_block = lax.dynamic_slice_in_dim(segment_ids, row_start, block_rows, 1)
        scores = (
            jnp.einsum("bqhd,bkhd->bhqk", query_block, key_rows, preferred_element_type=jnp.float32)
            * score_scale
        )
        allowed = segment_block[:, None, :, None] == segment_ids[:, None, None, :]
        return (jnp.where(allowed, scores, MASKED), query_block)

    def attend(block_index):
        scores, query_block = block_scores(block_index)
        row_max = jnp.max(scores, -1, keepdims=True)
        shifted = jnp.exp(scores - row_max)
        row_total = jnp.sum(shifted, -1, keepdims=True)
        attn_probs = (shifted / row_total).astype(jnp.bfloat16)
        context = jnp.einsum(
            "bhqk,bkhd->bqhd", attn_probs, value_rows, preferred_element_type=jnp.float32
        ).astype(jnp.bfloat16)
        return (context, (row_max + jnp.log(row_total))[..., 0])

    contexts, log_sums = lax.map(attend, jnp.arange(block_count))
    context_rows = jnp.moveaxis(contexts, 0, 1).reshape(seq_count, length, local_width)
    attn_part = jnp.einsum(
        "ble,de->bld", context_rows, out_full, preferred_element_type=jnp.float32
    )
    norm_all, attn_sum = exchange(mesh, 2, gather=(norm_here,), scatter=(split(attn_part),))
    attn_sum = attn_sum.reshape(tokens.shape)
    norm_all = norm_all.reshape(n, m, -1)[:, :, 2 * bias_len + hid_len : small_len]
    vector_rows = norm_all.reshape(n, m, 6, vec_len).transpose(2, 1, 0, 3).reshape(6, -1)
    first_sum = tokens.astype(jnp.float32) + attn_sum + vector_rows[0]
    normed_one, unit_one, inv_one = layer_norm(first_sum, vector_rows[1], vector_rows[2])
    (normed_all,) = exchange(mesh, 3, gather=(pieces_of(normed_one.astype(jnp.bfloat16)),))
    normed_full = whole(normed_all)
    hidden_pre = (
        jnp.einsum("bld,df->blf", normed_full, in_full, preferred_element_type=jnp.float32)
        + hidden_full
    )
    activated, gelu_slope = gelu_parts(hidden_pre)
    act_low = activated.astype(jnp.bfloat16)
    mlp_part = jnp.einsum("blf,df->bld", act_low, down_full, preferred_element_type=jnp.float32)
    (mlp_sum,) = exchange(mesh, 4, scatter=(split(mlp_part),))
    mlp_sum = mlp_sum.reshape(tokens.shape)
    second_sum = normed_one + mlp_sum + vector_rows[3]
    normed_two, unit_two, inv_two = layer_norm(second_sum, vector_rows[4], vector_rows[5])
    layer_out = normed_two.astype(jnp.bfloat16)
    upstream = cotangent.astype(jnp.float32)
    grad_second = norm_back(upstream, unit_two, inv_two, vector_rows[4])
    (grad_mlp_all,) = exchange(mesh, 3, gather=(pieces_of(grad_second.astype(jnp.bfloat16)),))
    grad_mlp_full = whole(grad_mlp_all)
    down_grad = jnp.einsum(
        "bld,blf->df", grad_mlp_full, act_low, preferred_element_type=jnp.float32
    )
    grad_hidden = (
        jnp.einsum("bld,df->blf", grad_mlp_full, down_full, preferred_element_type=jnp.float32)
        * gelu_slope
    )
    hidden_low = grad_hidden.astype(jnp.bfloat16)
    hidden_grad = jnp.sum(grad_hidden, (0, 1))[None]
    in_grad = jnp.einsum("bld,blf->df", normed_full, hidden_low, preferred_element_type=jnp.float32)
    back_part = jnp.einsum("blf,df->bld", hidden_low, in_full, preferred_element_type=jnp.float32)
    (back_sum,) = exchange(mesh, 4, scatter=(split(back_part),))
    grad_normed = grad_second + back_sum.reshape(tokens.shape)
    grad_first = norm_back(grad_normed, unit_one, inv_one, vector_rows[1])
    vector_grad = jnp.stack(
        [
            jnp.sum(grad_first, (0, 1)),
            jnp.sum(grad_normed * unit_one, (0, 1)),
            jnp.sum(grad_normed, (0, 1)),
            jnp.sum(grad_second, (0, 1)),
            jnp.sum(upstream * unit_two, (0, 1)),
            jnp.sum(upstream, (0, 1)),
        ]
    )
    vector_tile = jnp.pad(vector_grad, ((0, 2), (0, 0)))[None]
    grad_attn_all, vector_all = exchange(
        mesh, 5, gather=(pieces_of(grad_first.astype(jnp.bfloat16)), vector_tile)
    )
    grad_attn_full = whole(grad_attn_all)
    vector_sum = jnp.sum(vector_all[:, 0, :6], 0).reshape(6, m, n, vec_len)
    vector_here = lax.dynamic_index_in_dim(vector_sum, lax.axis_index("tensor"), 2, keepdims=False)
    out_grad = jnp.einsum(
        "bld,ble->de", grad_attn_full, context_rows, preferred_element_type=jnp.float32
    )
    grad_context = jnp.einsum(
        "bld,de->ble", grad_attn_full, out_full, preferred_element_type=jnp.float32
    ).astype(jnp.bfloat16)
    grad_heads = grad_context.reshape(head_shape)
    row_delta = jnp.sum(
        grad_heads.astype(jnp.float32) * context_rows.reshape(head_shape).astype(jnp.float32), -1
    )

    def backward_block(running, block_index):
        key_grad, value_grad = running
        scores, query_block = block_scores(block_index)
        row_start = block_index * block_rows
        grad_block = lax.dynamic_slice_in_dim(grad_heads, row_start, block_rows, 1)
        delta_block = lax.dynamic_slice_in_dim(row_delta, row_start, block_rows, 1)
        probs_again = jnp.exp(scores - log_sums[block_index][..., None])
        probs_low = probs_again.astype(jnp.bfloat16)
        value_grad = value_grad + jnp.einsum(
            "bhqk,bqhd->bkhd", probs_low, grad_block, preferred_element_type=jnp.float32
        )
        grad_probs = jnp.einsum(
            "bqhd,bkhd->bhqk", grad_block, value_rows, preferred_element_type=jnp.float32
        )
        grad_scores = (
            probs_again * (grad_probs - jnp.transpose(delta_block, (0, 2, 1))[..., None])
        ).astype(jnp.bfloat16)
        query_grad = (
            jnp.einsum("bhqk,bkhd->bqhd", grad_scores, key_rows, preferred_element_type=jnp.float32)
            * score_scale
        )
        key_grad = (
            key_grad
            + jnp.einsum(
                "bhqk,bqhd->bkhd", grad_scores, query_block, preferred_element_type=jnp.float32
            )
            * score_scale
        )
        return ((key_grad, value_grad), query_grad)

    zero_heads = jnp.zeros(head_shape, jnp.float32)
    (key_grad, value_grad), query_grads = lax.scan(
        backward_block, (zero_heads, zero_heads), jnp.arange(block_count)
    )
    query_grad = jnp.moveaxis(query_grads, 0, 1).reshape(seq_count, length, local_width)
    key_grad = key_grad.reshape(seq_count, length, local_width)
    value_grad = value_grad.reshape(seq_count, length, local_width)
    bias_grad = jnp.stack([jnp.sum(query_grad, (0, 1)), jnp.sum(value_grad, (0, 1))])
    grads_low = jnp.concatenate([query_grad, key_grad, value_grad], -1).astype(jnp.bfloat16)
    qkv_grad = jnp.einsum("bld,ble->de", full_tokens, grads_low, preferred_element_type=jnp.float32)
    token_part = jnp.einsum("ble,de->bld", grads_low, qkv_full, preferred_element_type=jnp.float32)
    grads = [
        g.astype(jnp.bfloat16).reshape(m, share, -1) for g in (qkv_grad, out_grad, in_grad, down_grad)
    ]
    small_grads = jnp.concatenate(
        [
            bias_grad.reshape(2, m, bias_len).transpose(1, 0, 2).reshape(m, -1),
            hidden_grad.reshape(m, hid_len),
            vector_here.transpose(1, 0, 2).reshape(m, -1),
        ],
        axis=1,
    )
    small_grads = jnp.pad(small_grads, ((0, 0), (0, tile * 128 - small_len))).reshape(m, tile, 128)
    token_sum, qkv_sum, out_sum, in_shard, down_sum, small_sum = exchange(
        mesh, 6, scatter=(split(token_part),), wide_scatter=(*grads, small_grads)
    )
    tokens_grad = (grad_first + token_sum.reshape(tokens.shape)).astype(jnp.bfloat16)
    qkv_shard = jnp.stack([qkv_sum[:, c * part : (c + 1) * part] for c in range(3)])
    out_shard = out_sum.T
    down_shard = down_sum.T
    small_sum = small_sum.reshape(-1)
    bias_shard = small_sum[: 2 * bias_len].reshape(qv_bias.shape)
    hidden_shard = small_sum[2 * bias_len : 2 * bias_len + hid_len].reshape(hidden_bias.shape)
    vectors_grad = small_sum[2 * bias_len + hid_len : small_len].reshape(norm_vectors.shape)
    return (
        layer_out,
        tokens_grad,
        qkv_shard,
        out_shard,
        in_shard,
        down_shard,
        bias_shard,
        hidden_shard,
        vectors_grad,
    )


def solution(mesh):
    return jax.shard_map(
        functools.partial(local, mesh),
        mesh=mesh,
        in_specs=(
            P("dp", "tensor", None),
            P("dp", None),
            P(None, "dp", "tensor"),
            P("tensor", "dp"),
            P("dp", "tensor"),
            P("tensor", "dp"),
            P(None, "tensor", "dp"),
            P("tensor", "dp"),
            P(None, ("dp", "tensor")),
            P("dp", "tensor", None),
        ),
        out_specs=(
            P("dp", "tensor", None),
            P("dp", "tensor", None),
            P(None, "dp", "tensor"),
            P("tensor", "dp"),
            P("dp", "tensor"),
            P("tensor", "dp"),
            P(None, "tensor", "dp"),
            P("tensor", "dp"),
            P(None, ("dp", "tensor")),
        ),
        check_vma=False,
    )
```

```python
import functools
import itertools
import jax
import jax.numpy as jnp
from jax import lax
from jax.experimental import pallas as pl
from jax.experimental.pallas import tpu as pltpu
from jax.sharding import PartitionSpec as P

DH = 64


EPS = 1e-05
MASKED = -1e30
MESH_ID = pl.DeviceIdType.MESH


def remote(src, dst, send_sem, recv_sem, where):
    return pltpu.make_async_remote_copy(
        src_ref=src, dst_ref=dst, send_sem=send_sem, recv_sem=recv_sem,
        device_id=where, device_id_type=MESH_ID)


def line_gather(n, pieces, x, out, send, recv, own):
    me = lax.axis_index("tensor")
    right, left = {"tensor": me + 1}, {"tensor": me - 1}

    def copy(way, step, c, shard, to):
        src = x.at[c] if step == 0 else out.at[shard, c]
        return remote(src, out.at[shard, c], send.at[way, step, c], recv.at[way, step, c], to)

    def landed(way, step, c, shard):
        to = right if way == 0 else left
        remote(out.at[shard, c], out.at[shard, c], send.at[way, step, c], recv.at[way, step, c], to).wait_recv()

    def stage(step):
        if step == 0:
            pltpu.make_async_copy(x, out.at[me], own).start()
        for c in range(pieces):
            if step > 0:
                pl.when(me - step >= 0)(lambda: landed(0, step - 1, c, me - step))
                pl.when(me + step <= n - 1)(lambda: landed(1, step - 1, c, me + step))
            if step < n - 1:
                pl.when((me < n - 1) & (me - step >= 0))(lambda: copy(0, step, c, me - step, right).start())
                pl.when((me > 0) & (me + step <= n - 1))(lambda: copy(1, step, c, me + step, left).start())

    def finish():
        pltpu.make_async_copy(x, out.at[me], own).wait()
        for step in range(n - 1):
            for c in range(pieces):
                pl.when((me < n - 1) & (me - step >= 0))(lambda: copy(0, step, c, me - step, right).wait_send())
                pl.when((me > 0) & (me + step <= n - 1))(lambda: copy(1, step, c, me + step, left).wait_send())

    return [functools.partial(stage, s) for s in range(n)] + [finish]


def line_scatter(n, pieces, p, out, got, acc, send, recv):
    me = lax.axis_index("tensor")
    right, left = {"tensor": me + 1}, {"tensor": me - 1}

    def copy(way, t, c):
        return remote(acc.at[way, t, c], got.at[way, t, c], send.at[way, t, c], recv.at[way, t, c],
                      right if way == 0 else left)

    def push(way, t, c, d):
        first = me == 0 if way == 0 else me == n - 1

        @pl.when(first)
        def _():
            acc[way, t, c] = p[d, c]

        @pl.when(jnp.logical_not(first))
        def _():
            copy(way, t, c).wait_recv()
            acc[way, t, c] = (p[d, c].astype(jnp.float32) + got[way, t, c].astype(jnp.float32)).astype(acc.dtype)

        copy(way, t, c).start()

    def stage(t):
        for c in range(pieces):
            pl.when(n - 1 - t > me)(lambda: push(0, t, c, n - 1 - t))
            pl.when(t < me)(lambda: push(1, t, c, t))

    def take(way, t, c):
        copy(way, t, c).wait_recv()
        out[c] += got[way, t, c].astype(jnp.float32)

    def finish():
        for c in range(pieces):
            out[c] = p[me, c].astype(jnp.float32)
        for t in range(n - 1):
            for c in range(pieces):
                pl.when((me > 0) & (n - 1 - t == me))(lambda: take(0, t, c))
                pl.when((me < n - 1) & (t == me))(lambda: take(1, t, c))
        for t in range(n - 1):
            for c in range(pieces):
                pl.when(n - 1 - t > me)(lambda: copy(0, t, c).wait_send())
                pl.when(t < me)(lambda: copy(1, t, c).wait_send())

    return [functools.partial(stage, t) for t in range(n - 1)] + [finish]


def pair_place(n):
    me = lax.axis_index("dp")
    core = lax.rem(me, 2)
    chip = (me - core) // 2
    twin = {"dp": me + 1 - 2 * core}
    return me, core, chip, twin


def group_gather(n, x, out, send, recv, fsend, frecv, own):
    me, core, chip, twin = pair_place(n)
    chips = n // 2

    def far(j):
        to = lax.rem(chip + j, chips) * 2 + core
        return remote(x, out.at[me], send.at[j], recv.at[j], {"dp": to})

    def source(j):
        return lax.rem(chip - j + chips, chips) * 2 + core

    def near(j):
        at = source(j)
        return remote(x if j == 0 else out.at[at], out.at[at], fsend.at[j], frecv.at[j], twin)

    def landed(j, at, sem_s, sem_r):
        remote(out.at[at], out.at[at], sem_s.at[j], sem_r.at[j], twin).wait_recv()

    def begin():
        for j in range(1, chips):
            far(j).start()
        near(0).start()
        pltpu.make_async_copy(x, out.at[me], own).start()

    def relay():
        for j in range(1, chips):
            landed(j, source(j), send, recv)
            near(j).start()

    def finish():
        for j in range(chips):
            landed(j, source(j) + 1 - 2 * core, fsend, frecv)
            near(j).wait_send()
        for j in range(1, chips):
            far(j).wait_send()
        pltpu.make_async_copy(x, out.at[me], own).wait()

    return [begin, relay, finish]


def group_scatter(n, g, out, tgot, both, fgot, send, recv, fsend, frecv):
    me, core, chip, twin = pair_place(n)
    chips = n // 2

    def near(j):
        to = lax.rem(chip + j, chips)
        return remote(g.at[to * 2 + 1 - core], tgot.at[j], fsend.at[j], frecv.at[j], twin)

    def far(j):
        to = lax.rem(chip + j, chips) * 2 + core
        return remote(both.at[j], fgot.at[j], send.at[j], recv.at[j], {"dp": to})

    order = list(range(1, chips)) + [0]

    def begin():
        for j in order:
            near(j).start()

    def spread():
        for j in order:
            near(j).wait_recv()
            mine = lax.rem(chip + j, chips) * 2 + core
            total = g[mine].astype(jnp.float32) + tgot[j].astype(jnp.float32)
            if j == 0:
                out[...] = total
            else:
                both[j] = total.astype(both.dtype)
                far(j).start()

    def finish():
        for j in range(1, chips):
            far(j).wait_recv()
            out[...] += fgot[j].astype(jnp.float32)
        for j in range(chips):
            near(j).wait_send()
        for j in range(1, chips):
            far(j).wait_send()

    return [begin, spread, finish]


def exchange(mesh, ident, gather=(), scatter=(), wide_gather=(), wide_scatter=()):
    n, m = mesh.shape["tensor"], mesh.shape["dp"]
    dma = pltpu.SemaphoreType.DMA
    vmem = pl.BlockSpec(memory_space=pltpu.VMEM)
    outs, specs, scratch, groups = [], [], [], []
    for x in gather:
        outs.append(jax.ShapeDtypeStruct((n,) + x.shape, x.dtype))
        specs.append(pl.BlockSpec(memory_space=pl.ANY))
        own = [dma((2, n - 1, x.shape[0])), dma((2, n - 1, x.shape[0])), dma]
        groups.append((functools.partial(line_gather, n, x.shape[0]), len(own)))
        scratch += own
    for x in scatter:
        outs.append(jax.ShapeDtypeStruct(x.shape[1:], jnp.float32))
        specs.append(vmem)
        slots = (2, n - 1) + x.shape[1:]
        own = [pltpu.VMEM(slots, x.dtype)] * 2 + [dma((2, n - 1, x.shape[1]))] * 2
        groups.append((functools.partial(line_scatter, n, x.shape[1]), len(own)))
        scratch += own
    for x in wide_gather:
        outs.append(jax.ShapeDtypeStruct((m,) + x.shape, x.dtype))
        specs.append(pl.BlockSpec(memory_space=pl.ANY))
        own = [dma((m // 2,))] * 4 + [dma]
        groups.append((functools.partial(group_gather, m), len(own)))
        scratch += own
    for x in wide_scatter:
        outs.append(jax.ShapeDtypeStruct(x.shape[1:], jnp.float32))
        specs.append(vmem)
        own = [pltpu.VMEM((m // 2,) + x.shape[1:], x.dtype)] * 3 + [dma((m // 2,))] * 4
        groups.append((functools.partial(group_scatter, m), len(own)))
        scratch += own
    operands = list(gather) + list(scatter) + list(wide_gather) + list(wide_scatter)
    count = len(operands)

    def kernel(*refs):
        ins, results, rest = refs[:count], refs[count:2 * count], list(refs[2 * count:])
        barrier = pltpu.get_barrier_semaphore()
        me = lax.axis_index("tensor")

        def greet(where):
            pl.semaphore_signal(barrier, inc=1, device_id=where, device_id_type=MESH_ID)

        if gather or scatter:
            pl.when(me > 0)(lambda: greet({"tensor": me - 1}))
            pl.when(me < n - 1)(lambda: greet({"tensor": me + 1}))
        if wide_gather or wide_scatter:
            _, core, chip, twin = pair_place(m)
            greet(twin)
            for j in range(1, m // 2):
                greet({"dp": lax.rem(chip + j, m // 2) * 2 + core})
        peers = m // 2 if wide_gather or wide_scatter else 0
        if gather or scatter:
            peers = peers + (me > 0).astype(jnp.int32) + (me < n - 1).astype(jnp.int32)
        pl.semaphore_wait(barrier, peers)
        plans = []
        for i, (make, size) in enumerate(groups):
            own, rest = rest[:size], rest[size:]
            plans.append(make(ins[i], results[i], *own))
        lines = plans[: len(gather) + len(scatter)][::-1]
        wides = plans[len(lines) :][::-1]
        run_stage = [lambda p=p: p[0]() for p in wides] + [lambda p=p: p[0]() for p in lines]
        middle = [p[1] for p in wides]
        along = [stage for row in itertools.zip_longest(*[p[1:-1] for p in lines]) for stage in row if stage]
        run_stage += along[:-1] + middle + along[-1:] if wide_gather else middle + along
        run_stage += [p[-1] for p in lines] + [p[-1] for p in wides]
        for stage in run_stage:
            stage()

    return pl.pallas_call(
        kernel, out_shape=tuple(outs), in_specs=[vmem] * count, out_specs=tuple(specs),
        scratch_shapes=scratch, name=f"exchange_{ident}",
        compiler_params=pltpu.CompilerParams(
            collective_id=ident, has_side_effects=True, vmem_limit_bytes=48 * 1024 * 1024),
    )(*operands)


PIECES = 2

def layer_norm(summed, gain, shift):
    center = summed - jnp.mean(summed, -1, keepdims=True)
    inv_std = lax.rsqrt(jnp.mean(center * center, -1, keepdims=True) + EPS)
    normed = center * inv_std
    return (normed * gain + shift, normed, inv_std)


def norm_back(upstream, normed, inv_std, gain):
    scaled = upstream * gain
    return inv_std * (
        scaled
        - jnp.mean(scaled, -1, keepdims=True)
        - normed * jnp.mean(scaled * normed, -1, keepdims=True)
    )


def gelu_parts(inputs):
    cdf_part = 0.5 * (1.0 + lax.erf(inputs * 0.7071067811865476))
    return (
        inputs * cdf_part,
        cdf_part + inputs * jnp.exp(-0.5 * inputs * inputs) * 0.3989422804014327,
    )


def local(
    mesh,
    tokens,
    segment_ids,
    qkv_weight,
    out_weight,
    in_weight,
    down_weight,
    qv_bias,
    hidden_bias,
    norm_vectors,
    cotangent,
):
    n, m = mesh.shape["tensor"], mesh.shape["dp"]
    seq_count, rows, width = tokens.shape
    share = qkv_weight.shape[1]
    part = qkv_weight.shape[2]
    hidden = in_weight.shape[1]
    qkv_cols = 3 * part
    marks = (qkv_cols, qkv_cols + part, qkv_cols + part + hidden)
    packed = jnp.concatenate(
        [qkv_weight[0], qkv_weight[1], qkv_weight[2], out_weight.T, in_weight, down_weight.T], axis=1
    )
    bias_len, hid_len = qv_bias.shape[2], hidden_bias.shape[1]
    vec_len = norm_vectors.shape[1]
    small = jnp.concatenate(
        [qv_bias.astype(jnp.float32).reshape(-1), hidden_bias.astype(jnp.float32).reshape(-1), norm_vectors.reshape(-1)]
    )
    small_len = small.shape[0]
    tile = -(-small_len // 1024) * 8
    small = jnp.pad(small, (0, tile * 128 - small_len)).reshape(tile, 128)

    def pieces_of(rows_in):
        return rows_in.reshape(PIECES, -1, width)

    def split(part_rows):
        return part_rows.astype(jnp.bfloat16).reshape(n, PIECES, -1, width)

    def whole(gathered):
        return gathered.reshape(seq_count, -1, width)

    tokens_all, packed_all, small_all = exchange(
        mesh, 1, gather=(pieces_of(tokens),), wide_gather=(packed, small)
    )
    full_tokens = whole(tokens_all)
    weights = packed_all.reshape(m * share, -1)
    qkv_full = weights[:, : marks[0]]
    out_full, in_full, down_full = (
        weights[:, marks[0] : marks[1]],
        weights[:, marks[1] : marks[2]],
        weights[:, marks[2] :],
    )
    small_all = small_all.reshape(m, -1)
    qv_full = small_all[:, : 2 * bias_len].reshape(m, 2, bias_len).transpose(1, 0, 2).reshape(2, -1)
    hidden_full = small_all[:, 2 * bias_len : 2 * bias_len + hid_len].reshape(-1)
    norm_here = small_all.reshape(1, -1, 128)
    length = full_tokens.shape[1]
    local_width = part
    heads_here = local_width // DH
    score_scale = DH ** (-0.5)
    block_rows = min(512, length)
    block_count = length // block_rows
    head_shape = (seq_count, length, heads_here, DH)
    flat = jnp.einsum("bld,de->ble", full_tokens, qkv_full, preferred_element_type=jnp.float32)
    projected = [flat[..., c * part : (c + 1) * part] for c in range(3)]
    queries = (projected[0] + qv_full[0]).astype(jnp.bfloat16).reshape(head_shape)
    key_rows = projected[1].astype(jnp.bfloat16).reshape(head_shape)
    value_rows = (projected[2] + qv_full[1]).astype(jnp.bfloat16).reshape(head_shape)

    def block_scores(block_index):
        row_start = block_index * block_rows
        query_block = lax.dynamic_slice_in_dim(queries, row_start, block_rows, 1)
        segment_block = lax.dynamic_slice_in_dim(segment_ids, row_start, block_rows, 1)
        scores = (
            jnp.einsum("bqhd,bkhd->bhqk", query_block, key_rows, preferred_element_type=jnp.float32)
            * score_scale
        )
        allowed = segment_block[:, None, :, None] == segment_ids[:, None, None, :]
        return (jnp.where(allowed, scores, MASKED), query_block)

    def attend(block_index):
        scores, query_block = block_scores(block_index)
        row_max = jnp.max(scores, -1, keepdims=True)
        shifted = jnp.exp(scores - row_max)
        row_total = jnp.sum(shifted, -1, keepdims=True)
        attn_probs = (shifted / row_total).astype(jnp.bfloat16)
        context = jnp.einsum(
            "bhqk,bkhd->bqhd", attn_probs, value_rows, preferred_element_type=jnp.float32
        ).astype(jnp.bfloat16)
        return (context, (row_max + jnp.log(row_total))[..., 0])

    contexts, log_sums = lax.map(attend, jnp.arange(block_count))
    context_rows = jnp.moveaxis(contexts, 0, 1).reshape(seq_count, length, local_width)
    attn_part = jnp.einsum(
        "ble,de->bld", context_rows, out_full, preferred_element_type=jnp.float32
    )
    norm_all, attn_sum = exchange(mesh, 2, gather=(norm_here,), scatter=(split(attn_part),))
    attn_sum = attn_sum.reshape(tokens.shape)
    norm_all = norm_all.reshape(n, m, -1)[:, :, 2 * bias_len + hid_len : small_len]
    vector_rows = norm_all.reshape(n, m, 6, vec_len).transpose(2, 1, 0, 3).reshape(6, -1)
    first_sum = tokens.astype(jnp.float32) + attn_sum + vector_rows[0]
    normed_one, unit_one, inv_one = layer_norm(first_sum, vector_rows[1], vector_rows[2])
    (normed_all,) = exchange(mesh, 3, gather=(pieces_of(normed_one.astype(jnp.bfloat16)),))
    normed_full = whole(normed_all)
    hidden_pre = (
        jnp.einsum("bld,df->blf", normed_full, in_full, preferred_element_type=jnp.float32)
        + hidden_full
    )
    activated, gelu_slope = gelu_parts(hidden_pre)
    act_low = activated.astype(jnp.bfloat16)
    mlp_part = jnp.einsum("blf,df->bld", act_low, down_full, preferred_element_type=jnp.float32)
    (mlp_sum,) = exchange(mesh, 4, scatter=(split(mlp_part),))
    mlp_sum = mlp_sum.reshape(tokens.shape)
    second_sum = normed_one + mlp_sum + vector_rows[3]
    normed_two, unit_two, inv_two = layer_norm(second_sum, vector_rows[4], vector_rows[5])
    layer_out = normed_two.astype(jnp.bfloat16)
    upstream = cotangent.astype(jnp.float32)
    grad_second = norm_back(upstream, unit_two, inv_two, vector_rows[4])
    (grad_mlp_all,) = exchange(mesh, 3, gather=(pieces_of(grad_second.astype(jnp.bfloat16)),))
    grad_mlp_full = whole(grad_mlp_all)
    down_grad = jnp.einsum(
        "bld,blf->df", grad_mlp_full, act_low, preferred_element_type=jnp.float32
    )
    grad_hidden = (
        jnp.einsum("bld,df->blf", grad_mlp_full, down_full, preferred_element_type=jnp.float32)
        * gelu_slope
    )
    hidden_low = grad_hidden.astype(jnp.bfloat16)
    hidden_grad = jnp.sum(grad_hidden, (0, 1))[None]
    in_grad = jnp.einsum("bld,blf->df", normed_full, hidden_low, preferred_element_type=jnp.float32)
    back_part = jnp.einsum("blf,df->bld", hidden_low, in_full, preferred_element_type=jnp.float32)
    (back_sum,) = exchange(mesh, 4, scatter=(split(back_part),))
    grad_normed = grad_second + back_sum.reshape(tokens.shape)
    grad_first = norm_back(grad_normed, unit_one, inv_one, vector_rows[1])
    vector_grad = jnp.stack(
        [
            jnp.sum(grad_first, (0, 1)),
            jnp.sum(grad_normed * unit_one, (0, 1)),
            jnp.sum(grad_normed, (0, 1)),
            jnp.sum(grad_second, (0, 1)),
            jnp.sum(upstream * unit_two, (0, 1)),
            jnp.sum(upstream, (0, 1)),
        ]
    )
    vector_tile = jnp.pad(vector_grad, ((0, 2), (0, 0)))[None]
    grad_attn_all, vector_all = exchange(
        mesh, 5, gather=(pieces_of(grad_first.astype(jnp.bfloat16)), vector_tile)
    )
    grad_attn_full = whole(grad_attn_all)
    vector_sum = jnp.sum(vector_all[:, 0, :6], 0).reshape(6, m, n, vec_len)
    vector_here = lax.dynamic_index_in_dim(vector_sum, lax.axis_index("tensor"), 2, keepdims=False)
    out_grad = jnp.einsum(
        "bld,ble->de", grad_attn_full, context_rows, preferred_element_type=jnp.float32
    )
    grad_context = jnp.einsum(
        "bld,de->ble", grad_attn_full, out_full, preferred_element_type=jnp.float32
    ).astype(jnp.bfloat16)
    grad_heads = grad_context.reshape(head_shape)
    row_delta = jnp.sum(
        grad_heads.astype(jnp.float32) * context_rows.reshape(head_shape).astype(jnp.float32), -1
    )

    def backward_block(running, block_index):
        key_grad, value_grad = running
        scores, query_block = block_scores(block_index)
        row_start = block_index * block_rows
        grad_block = lax.dynamic_slice_in_dim(grad_heads, row_start, block_rows, 1)
        delta_block = lax.dynamic_slice_in_dim(row_delta, row_start, block_rows, 1)
        probs_again = jnp.exp(scores - log_sums[block_index][..., None])
        probs_low = probs_again.astype(jnp.bfloat16)
        value_grad = value_grad + jnp.einsum(
            "bhqk,bqhd->bkhd", probs_low, grad_block, preferred_element_type=jnp.float32
        )
        grad_probs = jnp.einsum(
            "bqhd,bkhd->bhqk", grad_block, value_rows, preferred_element_type=jnp.float32
        )
        grad_scores = (
            probs_again * (grad_probs - jnp.transpose(delta_block, (0, 2, 1))[..., None])
        ).astype(jnp.bfloat16)
        query_grad = (
            jnp.einsum("bhqk,bkhd->bqhd", grad_scores, key_rows, preferred_element_type=jnp.float32)
            * score_scale
        )
        key_grad = (
            key_grad
            + jnp.einsum(
                "bhqk,bqhd->bkhd", grad_scores, query_block, preferred_element_type=jnp.float32
            )
            * score_scale
        )
        return ((key_grad, value_grad), query_grad)

    zero_heads = jnp.zeros(head_shape, jnp.float32)
    (key_grad, value_grad), query_grads = lax.scan(
        backward_block, (zero_heads, zero_heads), jnp.arange(block_count)
    )
    query_grad = jnp.moveaxis(query_grads, 0, 1).reshape(seq_count, length, local_width)
    key_grad = key_grad.reshape(seq_count, length, local_width)
    value_grad = value_grad.reshape(seq_count, length, local_width)
    bias_grad = jnp.stack([jnp.sum(query_grad, (0, 1)), jnp.sum(value_grad, (0, 1))])
    grads_low = jnp.concatenate([query_grad, key_grad, value_grad], -1).astype(jnp.bfloat16)
    qkv_grad = jnp.einsum("bld,ble->de", full_tokens, grads_low, preferred_element_type=jnp.float32)
    token_part = jnp.einsum("ble,de->bld", grads_low, qkv_full, preferred_element_type=jnp.float32)
    grads = jnp.concatenate(
        [g.astype(jnp.bfloat16) for g in (qkv_grad, out_grad, in_grad, down_grad)], axis=1
    ).reshape(m, share, -1)
    small_grads = jnp.concatenate(
        [
            bias_grad.reshape(2, m, bias_len).transpose(1, 0, 2).reshape(m, -1),
            hidden_grad.reshape(m, hid_len),
            vector_here.transpose(1, 0, 2).reshape(m, -1),
        ],
        axis=1,
    )
    small_grads = jnp.pad(small_grads, ((0, 0), (0, tile * 128 - small_len))).reshape(m, tile, 128)
    token_sum, grad_sum, small_sum = exchange(
        mesh, 6, scatter=(split(token_part),), wide_scatter=(grads, small_grads)
    )
    tokens_grad = (grad_first + token_sum.reshape(tokens.shape)).astype(jnp.bfloat16)
    qkv_shard = jnp.stack([grad_sum[:, c * part : (c + 1) * part] for c in range(3)])
    out_shard = grad_sum[:, marks[0] : marks[1]].T
    in_shard = grad_sum[:, marks[1] : marks[2]]
    down_shard = grad_sum[:, marks[2] :].T
    small_sum = small_sum.reshape(-1)
    bias_shard = small_sum[: 2 * bias_len].reshape(qv_bias.shape)
    hidden_shard = small_sum[2 * bias_len : 2 * bias_len + hid_len].reshape(hidden_bias.shape)
    vectors_grad = small_sum[2 * bias_len + hid_len : small_len].reshape(norm_vectors.shape)
    return (
        layer_out,
        tokens_grad,
        qkv_shard,
        out_shard,
        in_shard,
        down_shard,
        bias_shard,
        hidden_shard,
        vectors_grad,
    )


def solution(mesh):
    return jax.shard_map(
        functools.partial(local, mesh),
        mesh=mesh,
        in_specs=(
            P("dp", "tensor", None),
            P("dp", None),
            P(None, "dp", "tensor"),
            P("tensor", "dp"),
            P("dp", "tensor"),
            P("tensor", "dp"),
            P(None, "tensor", "dp"),
            P("tensor", "dp"),
            P(None, ("dp", "tensor")),
            P("dp", "tensor", None),
        ),
        out_specs=(
            P("dp", "tensor", None),
            P("dp", "tensor", None),
            P(None, "dp", "tensor"),
            P("tensor", "dp"),
            P("dp", "tensor"),
            P("tensor", "dp"),
            P(None, "tensor", "dp"),
            P("tensor", "dp"),
            P(None, ("dp", "tensor")),
        ),
        check_vma=False,
    )
```
